32 devices in a mesh: seg: 2 (over y), chan: 8 (over z, x), band: 2 (over core).
Axes of the slice: x: 2, y: 2, z: 4, core: 2. Of those that a mesh axis runs over, the one named last changes fastest.
Arguments:
- strain: float32 [2048, 8, 3000], P(('seg', 'chan'), 'band'), parts along dimension 0, may hold values from -84 to 84
- offsets: int32 [16, 6], P(('seg', 'band')), parts along dimension 0, may hold values from 0 to 2000, as said below
- bins: int32 [256], replicated, may hold values from 1 to 499, as said below
Outputs:
- cross_spectra: bfloat16 [2048, 1024, 2, 256], P(('seg', 'chan'), None, None, 'band'), parts along dimension 0
The draws below stay inside these ranges and needn't reach their ends.
There are 2 independent parts, one for each index of `seg`. The reference program is written for one: setup_inputs(seed, part) draws one part's arguments, and reference() takes and returns one part's arrays. A program takes and returns all parts, laid end to end along the dimension named above; an argument that names none is the same for every part. Nothing has to cross between parts.
Inputs may be any that keep to these rules, and one draw needn't show every extreme that they name: `offsets`: each window lies inside its minute file. `bins`: ascending and distinct.
All inputs are finite; a program needn't handle non-finite values.
Results may differ from the reference program's by a relative error of at most 0.0062.
Values may be sent and summed in bfloat16 or wider, within the bound.
A program may use at most 320 MiB of HBM per device.

```python
import math
import jax
import jax.numpy as jnp
from jax import lax

CHANNELS = 1024
SAMPLES = 3000
WIN_LEN = 1000
WIN_FILE = 6
BINS = 256
GROUP = 128
REACH = 64
FILES = 8


def draw_strain(key, part):
    key_noise, key_color, key_envelope = jax.random.split(key, 3)
    noise_vals = jnp.clip(jax.random.normal(key_noise, (CHANNELS, FILES, SAMPLES + 1), jnp.float32), -4.0, 4.0)
    low_edge = 0.3
    high_edge = 3.0
    color_gain = jnp.exp(jax.random.uniform(key_color, (CHANNELS, 1, 1), jnp.float32, math.log(low_edge), math.log(high_edge)))
    envelope = jnp.exp(jax.random.uniform(key_envelope, (CHANNELS, FILES, SAMPLES // 100, 1), jnp.float32, math.log(0.3), math.log(3.0)))
    envelope = jnp.broadcast_to(envelope, (CHANNELS, FILES, SAMPLES // 100, 100)).reshape(CHANNELS, FILES, SAMPLES)
    current = noise_vals[:, :, 1:]
    previous = noise_vals[:, :, :-1]
    return (current + color_gain * (current - previous)) * envelope


def draw_offsets(key, part):
    key_values, key_lowpos, key_highpos = jax.random.split(key, 3)
    entries = FILES * WIN_FILE
    values = jax.random.randint(key_values, (entries,), 0, SAMPLES - WIN_LEN + 1, jnp.int32)
    low_pos = jax.random.randint(key_lowpos, (), 0, entries // 2, jnp.int32)
    high_pos = jax.random.randint(key_highpos, (), entries // 2, entries, jnp.int32)
    values = values.at[low_pos].set(0).at[high_pos].set(SAMPLES - WIN_LEN)
    return values.reshape(FILES, WIN_FILE)


def draw_bins(key, part):
    shuffled = jax.random.permutation(key, WIN_LEN // 2 - 3) + 2
    chosen = jnp.sort(shuffled[:BINS - 2]).astype(jnp.int32)
    first_bin = jnp.array([1], jnp.int32)
    last_bin = jnp.array([WIN_LEN // 2 - 1], jnp.int32)
    return jnp.concatenate([first_bin, chosen, last_bin])


def setup_inputs(seed: int = 0, part: int = 0) -> dict:
    arg_keys = jax.random.split(jax.random.key(seed), 4)
    own_keys = jax.random.split(jax.random.fold_in(arg_keys[3], part), 4)
    strain = draw_strain(jax.random.fold_in(jax.random.fold_in(arg_keys[3], part), 71), part)
    offsets = draw_offsets(jax.random.fold_in(jax.random.fold_in(arg_keys[3], part), 71), part)
    bins = draw_bins(jax.random.fold_in(arg_keys[3], 71), part)
    return dict(strain=strain, offsets=offsets, bins=bins)


def normalize(strain):
    width = 2 * REACH + 1
    magnitude = jnp.abs(strain)
    zero_val = jnp.zeros((), magnitude.dtype)
    running = lax.reduce_window(magnitude, zero_val, lax.add, (1, 1, width), (1, 1, 1), ((0, 0), (0, 0), (REACH, REACH)))
    unit_row = jnp.ones((strain.shape[2],), magnitude.dtype)
    counts = lax.reduce_window(unit_row, zero_val, lax.add, (width,), (1,), ((REACH, REACH),))
    return strain / (running / counts + 1e-06)

def cut_windows(normed, offsets):

    def one_file(rows, starts):
        return jax.vmap(lambda start_pos: lax.dynamic_slice_in_dim(rows, start_pos, WIN_LEN, 1))(starts)
    pieces = jax.vmap(one_file, in_axes=(1, 0))(normed, offsets.astype(jnp.int32))
    sample_pos = jnp.arange(WIN_LEN, dtype=jnp.float32)
    hann_taper = 0.5 - 0.5 * jnp.cos(2.0 * math.pi * (sample_pos + 0.5) / WIN_LEN)
    return (jnp.transpose(pieces, (2, 0, 1, 3)) * hann_taper).astype(jnp.bfloat16)

def make_table(bins):
    sample_idx = jnp.arange(WIN_LEN, dtype=jnp.int32)
    phase_idx = sample_idx[:, None] * bins.astype(jnp.int32)[None, :] % WIN_LEN
    angles = phase_idx.astype(jnp.float32) * (2.0 * math.pi / WIN_LEN)
    return jnp.concatenate([jnp.cos(angles), -jnp.sin(angles)], axis=1).astype(jnp.bfloat16)

def spectra(windows, table):
    flat_rows = windows.reshape(-1, WIN_LEN)
    result = jnp.dot(flat_rows, table, preferred_element_type=jnp.float32)
    return result.reshape(windows.shape[0], windows.shape[1] * windows.shape[2], 2, table.shape[1] // 2)

def whiten(spec):
    chan_rows, win_count, _, bin_count = spec.shape
    grouped = spec.reshape(chan_rows, win_count, 2, bin_count // GROUP, GROUP)
    power_mean = lax.optimization_barrier(jnp.mean(lax.optimization_barrier(jnp.sum(grouped * grouped, axis=2)), axis=-1, keepdims=True))
    gain_inv = lax.rsqrt(power_mean + 1e-06)[:, :, None]
    return (grouped * gain_inv).reshape(spec.shape).astype(jnp.bfloat16)

def reference(strain, offsets, bins):
    normed = normalize(strain)
    windows = cut_windows(normed, offsets)
    whitened = whiten(spectra(windows, make_table(bins)))
    whole_u = whitened.astype(jnp.float32)
    whole_v = jnp.stack([whole_u[:, :, 1], -whole_u[:, :, 0]], axis=2)
    win_count = whole_u.shape[1]
    block_rows = 64
    u_blocks = whole_u.reshape((-1, block_rows) + whole_u.shape[1:])
    v_blocks = whole_v.reshape((-1, block_rows) + whole_v.shape[1:])

    def one_block(operands):
        u_block, v_block = operands
        real_part = jnp.einsum('iwcf,jwcf->ijf', u_block, whole_u)
        imag_part = jnp.einsum('iwcf,jwcf->ijf', v_block, whole_u)
        return (jnp.stack([real_part, imag_part], axis=2) / win_count).astype(jnp.bfloat16)
    result = lax.map(one_block, (u_blocks, v_blocks))
    return result.reshape(whole_u.shape[0], whole_u.shape[0], 2, whole_u.shape[3])
```

```python
import functools
import math

import jax
import jax.numpy as jnp
from jax import lax
from jax.experimental import pallas as pl
from jax.experimental.pallas import tpu as pltpu
from jax.sharding import PartitionSpec as P

WIN_LEN = 1000
GROUP = 128
REACH = 64


def normalize(strain):
    samples = strain.shape[2]
    padded = jnp.pad(jnp.abs(strain), ((0, 0), (0, 0), (REACH, REACH)))
    total, reach = padded, 1
    while reach < 2 * REACH:
        total = total[:, :, : total.shape[2] - reach] + total[:, :, reach:]
        reach *= 2
    running = total[:, :, :samples] + padded[:, :, 2 * REACH :]
    pos = jnp.arange(samples)
    counts = jnp.minimum(pos + REACH, samples - 1) - jnp.maximum(pos - REACH, 0) + 1
    return strain / (running / counts.astype(strain.dtype) + 1e-06)


def cut_windows(normed, offsets):

    def one_file(rows, starts):
        return jax.vmap(lambda start_pos: lax.dynamic_slice_in_dim(rows, start_pos, WIN_LEN, 1))(
            starts
        )

    pieces = jax.vmap(one_file, in_axes=(1, 0))(normed, offsets)
    sample_pos = jnp.arange(WIN_LEN, dtype=jnp.float32)
    hann_taper = 0.5 - 0.5 * jnp.cos(2.0 * math.pi * (sample_pos + 0.5) / WIN_LEN)
    return (jnp.transpose(pieces, (2, 0, 1, 3)) * hann_taper).astype(jnp.bfloat16)


def make_table(bins):
    sample_idx = jnp.arange(WIN_LEN, dtype=jnp.int32)
    phase_idx = sample_idx[:, None] * bins[None, :] % WIN_LEN
    angles = phase_idx.astype(jnp.float32) * (2.0 * math.pi / WIN_LEN)
    return jnp.concatenate([jnp.cos(angles), -jnp.sin(angles)], axis=1).astype(jnp.bfloat16)


def spectra(windows, table):
    flat_rows = windows.reshape(-1, WIN_LEN)
    result = jnp.dot(flat_rows, table, preferred_element_type=jnp.float32)
    return result.reshape(
        windows.shape[0], windows.shape[1] * windows.shape[2], 2, table.shape[1] // 2
    )


def whiten(spec):
    chan_rows, win_count, _, bin_count = spec.shape
    grouped = spec.reshape(chan_rows, win_count, 2, bin_count // GROUP, GROUP)
    power_mean = jnp.mean(jnp.sum(grouped * grouped, axis=2), axis=-1, keepdims=True)
    gain_inv = lax.rsqrt(power_mean + 1e-06)[:, :, None]
    return (grouped * gain_inv).reshape(spec.shape).astype(jnp.bfloat16)


def cross_block(lhs_rows, other, win_count):
    products = jnp.einsum("iwcf,jwcf->ijf", lhs_rows, other, preferred_element_type=jnp.float32)
    chan_rows = lhs_rows.shape[0] // 2
    split_parts = products.reshape(2, chan_rows, other.shape[0], products.shape[2])
    return (jnp.transpose(split_parts, (1, 2, 0, 3)) / win_count).astype(jnp.bfloat16)


def on_any(strain, offsets, bins):
    normed = normalize(strain)
    windows = cut_windows(normed, offsets)
    band_count = lax.axis_size("band")
    bin_share = bins.shape[0] // band_count
    all_windows = lax.all_gather(windows, "band", axis=1, tiled=True)
    my_bins = lax.dynamic_slice_in_dim(bins, lax.axis_index("band") * bin_share, bin_share)
    whitened = whiten(spectra(all_windows, make_table(my_bins)))
    chan_rows = whitened.shape[0]
    win_count = whitened.shape[1]
    rotated = jnp.stack([whitened[:, :, 1], -whitened[:, :, 0]], axis=2)
    lhs_rows = jnp.concatenate([whitened, rotated], axis=0)
    chan_count = lax.axis_size("chan")
    col_count = chan_rows * chan_count
    blank_out = jnp.zeros((chan_rows, col_count, 2, bin_share), jnp.bfloat16)
    return lax.dynamic_update_slice_in_dim(
        blank_out,
        cross_block(lhs_rows, lax.all_gather(whitened, "chan", axis=0, tiled=True), win_count),
        jnp.int32(0),
        1,
    )


def round_up(size, step):
    return -(-size // step) * step


def spectra_kernel(samples, win_file, depth, offs_ref, strain_ref, hann_ref, table_ref, place_ref, out_ref, mags, normed):
    m = pl.program_id(0)
    rows = mags.shape[0]
    chans = mags.shape[1]
    mags[pl.ds(0, REACH), :] = jnp.zeros((REACH, chans), jnp.float32)
    mags[pl.ds(REACH, samples), :] = jnp.abs(strain_ref[0])
    mags[pl.ds(REACH + samples, rows - REACH - samples), :] = jnp.zeros(
        (rows - REACH - samples, chans), jnp.float32
    )
    first = mags[...]
    total = first
    reach = 1
    while reach < 2 * REACH:
        total = total + pltpu.roll(total, rows - reach, 0)
        reach *= 2
    total = (total + pltpu.roll(first, rows - reach, 0))[:samples]
    pos = lax.broadcasted_iota(jnp.int32, (samples, chans), 0)
    counts = jnp.minimum(pos + REACH, samples - 1) - jnp.maximum(pos - REACH, 0) + 1
    normed[pl.ds(0, samples), :] = strain_ref[0] / (total / counts.astype(jnp.float32) + 1e-06)
    spare = normed.shape[0] - samples
    normed[pl.ds(samples, spare), :] = jnp.zeros((spare, chans), jnp.float32)
    for k in range(win_file):
        window = (normed[pl.ds(offs_ref[m, k], depth), :] * hann_ref[...]).astype(jnp.bfloat16)
        spec = jnp.dot(table_ref[...], window, preferred_element_type=jnp.float32)
        for g in range(spec.shape[0] // (2 * GROUP)):
            part = spec[g * 2 * GROUP : (g + 1) * 2 * GROUP]
            power = jnp.sum(part * part, axis=0, keepdims=True) / GROUP
            part = part * lax.rsqrt(power + 1e-06)
            both = jnp.concatenate([part[:GROUP], part[GROUP:]], axis=1).astype(jnp.bfloat16)
            both = jnp.dot(both, place_ref[...], preferred_element_type=jnp.float32).astype(jnp.bfloat16)
            at = pl.ds(g * GROUP, GROUP)
            out_ref[0, k, at, :] = both[:, :chans]
            out_ref[1, k, at, :] = both[:, chans:]


def own_spectra(strain, offsets, bins, place):
    chans, files, samples = strain.shape
    win_file = offsets.shape[1]
    depth = round_up(WIN_LEN, 128)
    table = make_table(bins)
    parts = table.reshape(WIN_LEN, 2, bins.shape[0] // GROUP, GROUP)
    rows = jnp.transpose(parts, (2, 1, 3, 0)).reshape(2 * bins.shape[0], WIN_LEN)
    rows = jnp.pad(rows, ((0, 0), (0, depth - WIN_LEN)))
    sample_pos = jnp.arange(WIN_LEN, dtype=jnp.float32)
    taper = 0.5 - 0.5 * jnp.cos(2.0 * math.pi * (sample_pos + 0.5) / WIN_LEN)
    taper = jnp.broadcast_to(jnp.pad(taper, (0, depth - WIN_LEN))[:, None], (depth, chans))
    return pl.pallas_call(
        functools.partial(spectra_kernel, samples, win_file, depth),
        grid_spec=pltpu.PrefetchScalarGridSpec(
            num_scalar_prefetch=1,
            grid=(files,),
            in_specs=[
                pl.BlockSpec((1, samples, chans), lambda m, o: (m, 0, 0)),
                pl.BlockSpec((depth, chans), lambda m, o: (0, 0)),
                pl.BlockSpec((2 * bins.shape[0], depth), lambda m, o: (0, 0)),
                pl.BlockSpec(place.shape, lambda m, o: (0, 0)),
            ],
            out_specs=pl.BlockSpec((2, win_file, bins.shape[0], chans), lambda m, o: (0, m, 0, 0)),
            scratch_shapes=[
                pltpu.VMEM((round_up(samples + 2 * REACH, 8), chans), jnp.float32),
                pltpu.VMEM((round_up(samples - WIN_LEN + depth, 8), chans), jnp.float32),
            ],
        ),
        out_shape=jax.ShapeDtypeStruct(
            (2, files * win_file, bins.shape[0], chans), jnp.bfloat16
        ),
        compiler_params=pltpu.CompilerParams(vmem_limit_bytes=40 * 2**20),
        name="spectra",
    )(offsets, jnp.transpose(strain, (1, 2, 0)), taper, rows, place)


FSTEP = 16
ISTEP = 16
SPARE = 8


def turn_kernel(first_ref, second_ref, place_ref, out_ref):
    bins, wins, chans = first_ref.shape
    both = jnp.concatenate(
        [first_ref[...].reshape(bins * wins, chans), second_ref[...].reshape(bins * wins, chans)], axis=1
    )
    plain = lax.dot_general(both, place_ref[...], (((1,), (1,)), ((), ())), preferred_element_type=jnp.float32)
    plain = plain.reshape(bins, wins, 2 * chans)
    for q in range(bins):
        rows = jnp.concatenate([plain[q, :, :chans], plain[q, :, chans:]], axis=0)
        out_ref[q] = rows.T.astype(jnp.bfloat16)


def turn_own(first, second, place):
    bins, wins, chans = first.shape
    spec = pl.BlockSpec((FSTEP, wins, chans), lambda i: (i, 0, 0))
    return pl.pallas_call(
        turn_kernel,
        grid=(bins // FSTEP,),
        in_specs=[spec, spec, pl.BlockSpec(place.shape, lambda i: (0, 0))],
        out_specs=pl.BlockSpec((FSTEP, chans, 2 * wins), lambda i: (i, 0, 0)),
        out_shape=jax.ShapeDtypeStruct((bins, chans, 2 * wins), jnp.bfloat16),
        cost_estimate=pl.CostEstimate(flops=10**6, bytes_accessed=8 * 2**20, transcendentals=0),
        name="turn",
    )(first, second, place)


def cross_kernel(has_prior, slot_ref, lhs_ref, one_ref, two_ref, *rest):
    if has_prior:
        rest = rest[1:]
    out_ref, lhs, held, low, high, stage, in_sems, out_sems = rest
    bins, chans, depth = lhs.shape
    wins = depth // 2
    pitch = chans + SPARE

    def fetch(part):
        rows = pl.ds(part * FSTEP, FSTEP)
        return (
            pltpu.make_async_copy(lhs_ref.at[rows], lhs.at[rows], in_sems.at[0, part]),
            pltpu.make_async_copy(one_ref.at[rows], held.at[0, rows], in_sems.at[1, part]),
            pltpu.make_async_copy(two_ref.at[rows], held.at[1, rows], in_sems.at[2, part]),
        )

    for part in range(bins // FSTEP):
        for copy in fetch(part):
            copy.start()

    even = lax.broadcasted_iota(jnp.int32, (FSTEP * wins, chans), 1) % 2 == 0
    sign = jnp.where(even, 1.0, -1.0)

    @pl.loop(0, bins // FSTEP)
    def _(part):
        for copy in fetch(part):
            copy.wait()
        base = part * FSTEP
        mixed = []
        for side in range(2):
            rows = held[side, pl.ds(base, FSTEP)].reshape(FSTEP * wins, chans).astype(jnp.float32)
            top = (rows * sign).astype(jnp.bfloat16).reshape(FSTEP, wins, chans)
            swapped = jnp.where(even, pltpu.roll(rows, chans - 1, 1), pltpu.roll(rows, 1, 1))
            mixed.append(
                jnp.concatenate([top, swapped.astype(jnp.bfloat16).reshape(FSTEP, wins, chans)], axis=1)
            )
        for q in range(FSTEP):
            rhs = jnp.concatenate([mixed[0][q], mixed[1][q]], axis=1)
            prod = jnp.dot(lhs[base + q], rhs, preferred_element_type=jnp.float32) * (1.0 / wins)
            at = pl.ds(pl.multiple_of((base + q) * pitch, 8), chans)
            low[at, :] = prod[:, :chans]
            high[at, :] = prod[:, chans:]

    def store(number, turn):
        return [
            pltpu.make_async_copy(
                stage.at[turn, side],
                out_ref.at[
                    pl.ds(number * ISTEP, ISTEP), pl.ds(pl.multiple_of(slot_ref[side] * chans, chans), chans)
                ],
                out_sems.at[turn, side],
            )
            for side in range(2)
        ]

    steps = chans // ISTEP

    @pl.loop(0, steps)
    def _(number):
        turn = lax.rem(number, 2)

        @pl.when(number >= 2)
        def _():
            for copy in store(number - 2, turn):
                copy.wait()

        for side, total in enumerate((low, high)):
            for q in range(ISTEP):
                rows = total[pl.ds(number * ISTEP + q, bins, stride=pitch), :]
                stage[turn, side, q] = rows.T.astype(jnp.bfloat16)
        for copy in store(number, turn):
            copy.start()

    for number in (steps - 2, steps - 1):
        for copy in store(number, number % 2):
            copy.wait()


def cross_step(lhs, prior, one, two, slots, blocks):
    bins, chans, depth = lhs.shape
    operands = [jnp.stack(slots).astype(jnp.int32), lhs, one, two]
    aliases = {}
    if prior is not None:
        aliases = {len(operands): 0}
        operands.append(prior)
    return pl.pallas_call(
        functools.partial(cross_kernel, prior is not None),
        in_specs=[pl.BlockSpec(memory_space=pltpu.SMEM)]
        + [pl.BlockSpec(memory_space=pl.ANY)] * (len(operands) - 1),
        out_specs=pl.BlockSpec(memory_space=pl.ANY),
        scratch_shapes=[
            pltpu.VMEM((bins, chans, depth), jnp.bfloat16),
            pltpu.VMEM((2, bins, depth // 2, chans), jnp.bfloat16),
            pltpu.VMEM((bins * (chans + SPARE), chans), jnp.float32),
            pltpu.VMEM((bins * (chans + SPARE), chans), jnp.float32),
            pltpu.VMEM((2, 2, ISTEP, chans, bins), jnp.bfloat16),
            pltpu.SemaphoreType.DMA((3, bins // FSTEP)),
            pltpu.SemaphoreType.DMA((2, 2)),
        ],
        out_shape=jax.ShapeDtypeStruct((chans, 2 * chans * blocks, bins), jnp.bfloat16),
        input_output_aliases=aliases,
        compiler_params=pltpu.CompilerParams(vmem_limit_bytes=48 * 2**20),
        cost_estimate=pl.CostEstimate(
            flops=4 * bins * depth * chans * chans,
            bytes_accessed=20 * 2**20,
            transcendentals=0,
        ),
        name="cross",
    )(*operands)


def own_halves(strain, offsets, bins, place):
    me = lax.axis_index("band")
    share = bins.shape[0] // 2
    mine = own_spectra(strain, offsets, bins, place)
    keep = lax.dynamic_slice_in_dim(mine, me * share, share, 2)
    sent = lax.dynamic_slice_in_dim(mine, (1 - me) * share, share, 2)
    other = lax.ppermute(sent, "band", [(0, 1), (1, 0)])
    joined = jnp.concatenate([keep, other], axis=1)
    turned = jnp.transpose(joined, (0, 2, 1, 3))
    return turned[0], turned[1]


def on_line(strain, offsets, bins):
    chans = strain.shape[0]
    col = jnp.arange(2 * chans)
    source = col // 2 + chans * (col % 2)
    place = (col[:, None] == source[None, :]).astype(jnp.bfloat16)
    a, b = own_halves(strain, offsets, bins, place)
    me = lax.axis_index("chan")
    z, x = me // 2, me % 2
    middle = (z == 1) | (z == 2)

    def along(value, pairs):
        return lax.ppermute(value, "chan", [(2 * p + s, 2 * q + s) for p, q in pairs for s in range(2)])

    def swap(value):
        return along(value, [(0, 1), (1, 0), (2, 3), (3, 2)])

    def outward(value):
        return along(value, [(1, 0), (2, 3)])

    def inner(value):
        return along(value, [(1, 2), (2, 1)])

    def across(value):
        return lax.ppermute(value, "chan", [(c, c ^ 1) for c in range(8)])

    def tie(*values):
        return lax.optimization_barrier(values)

    def choose(values):
        return jnp.where(z == 0, values[0], jnp.where(z == 1, values[1], jnp.where(z == 2, values[2], values[3])))

    near, mid, far = choose([1, 0, 3, 2]), choose([2, 2, 1, 1]), choose([3, 3, 0, 0])

    def slot(row, column, half):
        return 2 * (2 * row + column) + half

    def cross(prior, one, two, *slots):
        return cross_step(lhs, prior, one, two, slots, 8)

    near_a, in1_a, side_a, near_b, side_b = swap(a), inner(a), across(a), swap(b), across(b)
    lhs = turn_own(a, b, place)
    out = cross(None, a, b, slot(z, x, 0), slot(z, x, 1))
    near_a, in1_a, side_a, out = tie(near_a, in1_a, side_a, out)

    in1_b, out2_a, near_xa = inner(b), outward(in1_a), across(near_a)
    out = cross(out, side_a, near_a, slot(z, 1 - x, 0), slot(near, x, 0))
    near_b, side_b, in1_b, out = tie(near_b, side_b, in1_b, out)

    out2_b, in2_a, in2_b = outward(in1_b), inner(near_a), inner(near_b)
    out = cross(out, side_b, near_b, slot(z, 1 - x, 1), slot(near, x, 1))
    out2_a, near_xa, in2_a, out = tie(out2_a, near_xa, in2_a, out)

    mid_a = jnp.where(middle, in1_a, out2_a)
    mid_xa, out3_a = across(mid_a), outward(in2_a)
    out = cross(out, mid_a, near_xa, slot(mid, x, 0), slot(near, 1 - x, 0))
    out2_b, in2_b, out = tie(out2_b, in2_b, out)

    mid_b = jnp.where(middle, in1_b, out2_b)
    mid_xb, out3_b = across(mid_b), outward(in2_b)
    near_xb = swap(side_b)
    mid_xa, mid_b, out = tie(mid_xa, mid_b, out)
    out = cross(out, mid_b, mid_xa, slot(mid, x, 1), slot(mid, 1 - x, 0))
    out3_a, out = tie(out3_a, out)

    far_a = jnp.where(middle, in2_a, out3_a)
    far_xa = across(far_a)
    mid_xb, far_a, out = tie(mid_xb, far_a, out)
    out = cross(out, far_a, mid_xb, slot(far, x, 0), slot(mid, 1 - x, 1))
    out3_b, out = tie(out3_b, out)

    far_b = jnp.where(middle, in2_b, out3_b)
    far_xb = across(far_b)
    far_xa, far_b, out = tie(far_xa, far_b, out)
    out = cross(out, far_b, far_xa, slot(far, x, 1), slot(far, 1 - x, 0))
    near_xb, far_xb, out = tie(near_xb, far_xb, out)

    out = cross(out, near_xb, far_xb, slot(near, 1 - x, 1), slot(far, 1 - x, 1))
    return out.reshape(chans, 8 * chans, 2, bins.shape[0] // 2)


def on_device(strain, offsets, bins):
    if strain.shape[0] == 128 and lax.axis_size("chan") == 8 and bins.shape[0] // lax.axis_size("band") == 128:
        return on_line(strain, offsets, bins)
    return on_any(strain, offsets, bins)


def solution(mesh):
    placed = (P(("seg", "chan"), "band", None), P(("seg", "band"), None), P())
    return jax.shard_map(
        on_device,
        mesh=mesh,
        in_specs=placed,
        out_specs=P(("seg", "chan"), None, None, "band"),
        check_vma=False,
    )
```

```python
import functools
import math

import jax
import jax.numpy as jnp
from jax import lax
from jax.experimental import pallas as pl
from jax.experimental.pallas import tpu as pltpu
from jax.sharding import PartitionSpec as P

WIN_LEN = 1000
GROUP = 128
REACH = 64


def normalize(strain):
    samples = strain.shape[2]
    padded = jnp.pad(jnp.abs(strain), ((0, 0), (0, 0), (REACH, REACH)))
    total, reach = padded, 1
    while reach < 2 * REACH:
        total = total[:, :, : total.shape[2] - reach] + total[:, :, reach:]
        reach *= 2
    running = total[:, :, :samples] + padded[:, :, 2 * REACH :]
    pos = jnp.arange(samples)
    counts = jnp.minimum(pos + REACH, samples - 1) - jnp.maximum(pos - REACH, 0) + 1
    return strain / (running / counts.astype(strain.dtype) + 1e-06)


def cut_windows(normed, offsets):

    def one_file(rows, starts):
        return jax.vmap(lambda start_pos: lax.dynamic_slice_in_dim(rows, start_pos, WIN_LEN, 1))(
            starts
        )

    pieces = jax.vmap(one_file, in_axes=(1, 0))(normed, offsets)
    sample_pos = jnp.arange(WIN_LEN, dtype=jnp.float32)
    hann_taper = 0.5 - 0.5 * jnp.cos(2.0 * math.pi * (sample_pos + 0.5) / WIN_LEN)
    return (jnp.transpose(pieces, (2, 0, 1, 3)) * hann_taper).astype(jnp.bfloat16)


def make_table(bins):
    sample_idx = jnp.arange(WIN_LEN, dtype=jnp.int32)
    phase_idx = sample_idx[:, None] * bins[None, :] % WIN_LEN
    angles = phase_idx.astype(jnp.float32) * (2.0 * math.pi / WIN_LEN)
    return jnp.concatenate([jnp.cos(angles), -jnp.sin(angles)], axis=1).astype(jnp.bfloat16)


def spectra(windows, table):
    flat_rows = windows.reshape(-1, WIN_LEN)
    result = jnp.dot(flat_rows, table, preferred_element_type=jnp.float32)
    return result.reshape(
        windows.shape[0], windows.shape[1] * windows.shape[2], 2, table.shape[1] // 2
    )


def whiten(spec):
    chan_rows, win_count, _, bin_count = spec.shape
    grouped = spec.reshape(chan_rows, win_count, 2, bin_count // GROUP, GROUP)
    power_mean = jnp.mean(jnp.sum(grouped * grouped, axis=2), axis=-1, keepdims=True)
    gain_inv = lax.rsqrt(power_mean + 1e-06)[:, :, None]
    return (grouped * gain_inv).reshape(spec.shape).astype(jnp.bfloat16)


def cross_block(lhs_rows, other, win_count):
    products = jnp.einsum("iwcf,jwcf->ijf", lhs_rows, other, preferred_element_type=jnp.float32)
    chan_rows = lhs_rows.shape[0] // 2
    split_parts = products.reshape(2, chan_rows, other.shape[0], products.shape[2])
    return (jnp.transpose(split_parts, (1, 2, 0, 3)) / win_count).astype(jnp.bfloat16)


def on_any(strain, offsets, bins):
    normed = normalize(strain)
    windows = cut_windows(normed, offsets)
    band_count = lax.axis_size("band")
    bin_share = bins.shape[0] // band_count
    all_windows = lax.all_gather(windows, "band", axis=1, tiled=True)
    my_bins = lax.dynamic_slice_in_dim(bins, lax.axis_index("band") * bin_share, bin_share)
    whitened = whiten(spectra(all_windows, make_table(my_bins)))
    chan_rows = whitened.shape[0]
    win_count = whitened.shape[1]
    rotated = jnp.stack([whitened[:, :, 1], -whitened[:, :, 0]], axis=2)
    lhs_rows = jnp.concatenate([whitened, rotated], axis=0)
    chan_count = lax.axis_size("chan")
    col_count = chan_rows * chan_count
    blank_out = jnp.zeros((chan_rows, col_count, 2, bin_share), jnp.bfloat16)
    return lax.dynamic_update_slice_in_dim(
        blank_out,
        cross_block(lhs_rows, lax.all_gather(whitened, "chan", axis=0, tiled=True), win_count),
        jnp.int32(0),
        1,
    )


def round_up(size, step):
    return -(-size // step) * step


BLOCK = 120


def fill_table(bins_ref, table):
    step = 8
    sample = lax.broadcasted_iota(jnp.int32, (step, table.shape[1]), 1)
    inside = sample < WIN_LEN
    sample = sample.astype(jnp.float32)
    per = GROUP // (2 * step)

    @pl.loop(0, bins_ref.shape[0] // (2 * step), unroll=4)
    def _(block):
        cos_rows, sin_rows = [], []
        for q in range(2):
            at = pl.multiple_of((2 * block + q) * step, step)
            product = bins_ref[pl.ds(at, step), :][:, :1] * sample
            quarter = jnp.floor(product * (4.0 / WIN_LEN) + 0.5)
            angle = (product - quarter * (WIN_LEN // 4)) * (2.0 * math.pi / WIN_LEN)
            square = angle * angle
            sin = angle * (1.0 + square * (-1 / 6 + square * (1 / 120 + square * (-1 / 5040 + square * (1 / 362880)))))
            cos = 1.0 + square * (-1 / 2 + square * (1 / 24 + square * (-1 / 720 + square * (1 / 40320))))
            quarter = quarter - 4.0 * jnp.floor(quarter * 0.25)
            odd = (quarter == 1.0) | (quarter == 3.0)
            real = jnp.where(odd, sin, cos)
            imag = jnp.where(odd, cos, sin)
            real = jnp.where((quarter == 1.0) | (quarter == 2.0), -real, real)
            imag = jnp.where(quarter >= 2.0, imag, -imag)
            cos_rows.append(jnp.where(inside, real, 0.0).astype(jnp.bfloat16))
            sin_rows.append(jnp.where(inside, imag, 0.0).astype(jnp.bfloat16))
        first = pl.multiple_of((block // per) * 2 * GROUP + lax.rem(block, per) * 2 * step, 2 * step)
        table[pl.ds(first, 2 * step), :] = jnp.concatenate(cos_rows, axis=0)
        table[pl.ds(first + GROUP, 2 * step), :] = jnp.concatenate(sin_rows, axis=0)


def sum_eight(low, rows, mags, eights):
    total, reach = mags[pl.ds(low, rows + 8), :], 1
    while reach < 8:
        total = total + pltpu.roll(total, rows + 8 - reach, 0)
        reach *= 2
    eights[pl.ds(low, rows), :] = total[:rows]


def sum_four(low, rows, step, source):
    return (source[pl.ds(low, rows), :] + source[pl.ds(low + step, rows), :]) + (
        source[pl.ds(low + 2 * step, rows), :] + source[pl.ds(low + 3 * step, rows), :]
    )


def normalize_block(low, rows, source, mags, wides, normed):
    samples, chans = source.shape
    total = sum_four(low, rows, 32, wides) + mags[pl.ds(low + 2 * REACH, rows), :]
    if low >= REACH and low + rows + REACH <= samples:
        mean = total * (1.0 / (2 * REACH + 1))
    else:
        pos = lax.broadcasted_iota(jnp.int32, (rows, chans), 0) + low
        counts = jnp.minimum(pos + REACH, samples - 1) - jnp.maximum(pos - REACH, 0) + 1
        mean = total / counts.astype(jnp.float32)
    normed[pl.ds(low, rows), :] = source[pl.ds(low, rows), :] / (mean + 1e-06)


def spectra_kernel(offs_ref, strain_ref, hann_ref, bins_ref, keep_a, keep_b, send_a, send_b, strain, mags, eights, wides, normed, table, sems):
    files, samples, chans = strain.shape
    win_file = offs_ref.shape[1]
    depth = table.shape[1]
    half = chans // 2
    copies = [pltpu.make_async_copy(strain_ref.at[m], strain.at[m], sems.at[m]) for m in range(files)]
    for copy in copies:
        copy.start()
    for m in range(2):
        tail = mags.shape[1] - REACH - samples
        mags[m, pl.ds(0, REACH), :] = jnp.zeros((REACH, chans), jnp.float32)
        mags[m, pl.ds(REACH + samples, tail), :] = jnp.zeros((tail, chans), jnp.float32)
    for m in range(files):
        spare = normed.shape[1] - samples
        normed[m, pl.ds(samples, spare), :] = jnp.zeros((spare, chans), jnp.float32)
    fill_table(bins_ref, table)

    def blocks(rows):
        return [(low, min(BLOCK, rows - low)) for low in range(0, rows, BLOCK)]

    def prepare(m):
        own, source = mags.at[m % 2], strain.at[m]

        def load():
            copies[m].wait()
            own[pl.ds(REACH, samples), :] = jnp.abs(source[...])

        def wide(low, rows):
            wides[pl.ds(low, rows), :] = sum_four(low, rows, 8, eights)

        return (
            [load]
            + [functools.partial(sum_eight, low, rows, own, eights) for low, rows in blocks(samples + 120)]
            + [functools.partial(wide, low, rows) for low, rows in blocks(samples + 96)]
            + [
                functools.partial(normalize_block, low, rows, source, own, wides, normed.at[m])
                for low, rows in blocks(samples)
            ]
        )

    for piece in prepare(0):
        piece()
    pairs = win_file // 2
    left = lax.broadcasted_iota(jnp.int32, (GROUP, chans), 1) < half
    for m in range(files):
        for pair in range(pairs):
            pieces = prepare(m + 1) if m + 1 < files else []
            for piece in pieces[len(pieces) * pair // pairs : len(pieces) * (pair + 1) // pairs]:
                piece()
            wins = [
                (normed[m, pl.ds(offs_ref[m, 2 * pair + e], depth), :] * hann_ref[...]).astype(jnp.bfloat16)
                for e in range(2)
            ]
            spec = jnp.dot(table[...], jnp.concatenate(wins, axis=1), preferred_element_type=jnp.float32)
            for g, (out_a, out_b) in enumerate(((keep_a, keep_b), (send_a, send_b))):
                part = spec[g * 2 * GROUP : (g + 1) * 2 * GROUP]
                power = jnp.sum(part * part, axis=0, keepdims=True) / GROUP
                part = part * lax.rsqrt(power + 1e-06)
                for e in range(2):
                    real = part[:GROUP, e * chans : (e + 1) * chans]
                    imag = part[GROUP:, e * chans : (e + 1) * chans]
                    at = m * win_file + 2 * pair + e
                    out_a[at] = jnp.where(left, real, pltpu.roll(imag, half, 1)).astype(jnp.bfloat16)
                    out_b[at] = jnp.where(left, pltpu.roll(real, half, 1), imag).astype(jnp.bfloat16)


def own_spectra(strain, offsets, bins):
    chans, files, samples = strain.shape
    wins = files * offsets.shape[1]
    depth = round_up(WIN_LEN, 128)
    sample_pos = jnp.arange(WIN_LEN, dtype=jnp.float32)
    taper = 0.5 - 0.5 * jnp.cos(2.0 * math.pi * (sample_pos + 0.5) / WIN_LEN)
    taper = jnp.broadcast_to(jnp.pad(taper, (0, depth - WIN_LEN))[:, None], (depth, chans))
    rows = jnp.broadcast_to(bins.astype(jnp.float32)[:, None], (bins.shape[0], 128))
    whole = pl.BlockSpec(memory_space=pltpu.VMEM)
    shape = jax.ShapeDtypeStruct((wins, GROUP, chans), jnp.bfloat16)
    return pl.pallas_call(
        spectra_kernel,
        in_specs=[pl.BlockSpec(memory_space=pltpu.SMEM), pl.BlockSpec(memory_space=pl.ANY), whole, whole],
        out_specs=[whole] * 4,
        scratch_shapes=[
            pltpu.VMEM((files, samples, chans), jnp.float32),
            pltpu.VMEM((2, round_up(samples + 2 * REACH, 8), chans), jnp.float32),
            pltpu.VMEM((samples + 120, chans), jnp.float32),
            pltpu.VMEM((samples + 96, chans), jnp.float32),
            pltpu.VMEM((files, round_up(samples - WIN_LEN + depth, 8), chans), jnp.float32),
            pltpu.VMEM((2 * bins.shape[0], depth), jnp.bfloat16),
            pltpu.SemaphoreType.DMA((files,)),
        ],
        out_shape=[shape] * 4,
        compiler_params=pltpu.CompilerParams(vmem_limit_bytes=48 * 2**20),
        name="spectra",
    )(offsets, jnp.transpose(strain, (1, 2, 0)), taper, rows)


FSTEP = 16
ISTEP = 32
SPARE = 8


def turn_kernel(first_ref, second_ref, out_ref):
    bins, wins, chans = first_ref.shape
    half = chans // 2
    left = lax.broadcasted_iota(jnp.int32, (wins, chans), 1) < half
    for q in range(bins):
        first = first_ref[q].astype(jnp.float32)
        second = second_ref[q].astype(jnp.float32)
        real = jnp.where(left, first, pltpu.roll(second, half, 1))
        imag = jnp.where(left, pltpu.roll(first, half, 1), second)
        out_ref[q] = jnp.concatenate([real, imag], axis=0).T.astype(jnp.bfloat16)


def turn_own(first, second):
    bins, wins, chans = first.shape
    spec = pl.BlockSpec((FSTEP, wins, chans), lambda i: (i, 0, 0))
    return pl.pallas_call(
        turn_kernel,
        grid=(bins // FSTEP,),
        in_specs=[spec, spec],
        out_specs=pl.BlockSpec((FSTEP, chans, 2 * wins), lambda i: (i, 0, 0)),
        out_shape=jax.ShapeDtypeStruct((bins, chans, 2 * wins), jnp.bfloat16),
        cost_estimate=pl.CostEstimate(flops=10**6, bytes_accessed=8 * 2**20, transcendentals=0),
        name="turn",
    )(first, second)


def cross_kernel(counts, has_prior, meta_ref, lhs_ref, *rest):
    sides = len(counts)
    groups = []
    for count in counts:
        groups.append(rest[:count])
        rest = rest[count:]
    if has_prior:
        rest = rest[1:]
    out_ref, held, total, stage, in_sems, out_sems = rest
    bins, chans, depth = lhs_ref.shape
    wins = depth // 2
    pitch = chans + SPARE
    parts = bins // FSTEP

    def rows_of(part):
        return pl.ds(part * FSTEP, FSTEP)

    def held_copy(side, ref, part):
        return pltpu.make_async_copy(ref.at[rows_of(part)], held.at[side, rows_of(part)], in_sems.at[side, part])

    for part in range(parts):
        for side, refs in enumerate(groups):
            if len(refs) == 1:
                held_copy(side, refs[0], part).start()
            for n, ref in enumerate(refs if len(refs) > 1 else ()):

                @pl.when(meta_ref[sides + side] == n)
                def _():
                    held_copy(side, ref, part).start()

    lane = lax.broadcasted_iota(jnp.int32, (FSTEP * wins, chans), 1)
    odd = lane % 2
    straight = lane // 2 + odd * (chans // 2)
    crossed = lane // 2 + (1 - odd) * (chans // 2)
    sign = (1 - 2 * odd).astype(jnp.float32)

    @pl.loop(0, parts)
    def _(part):
        base = part * FSTEP
        mixed = []
        for side in range(sides):
            held_copy(side, groups[side][0], part).wait()
            rows = held[side, pl.ds(base, FSTEP)].reshape(FSTEP * wins, chans).astype(jnp.float32)
            upper = jnp.take_along_axis(rows, straight, axis=1) * sign
            lower = jnp.take_along_axis(rows, crossed, axis=1)
            mixed.append(
                jnp.concatenate(
                    [piece.astype(jnp.bfloat16).reshape(FSTEP, wins, chans) for piece in (upper, lower)], axis=1
                )
            )
        for q in range(FSTEP):
            rhs = jnp.concatenate([piece[q] for piece in mixed], axis=1)
            prod = jnp.dot(lhs_ref[base + q], rhs, preferred_element_type=jnp.float32) * (1.0 / wins)
            at = pl.ds(pl.multiple_of((base + q) * pitch, 8), chans)
            for side in range(sides):
                total[side, at, :] = prod[:, side * chans : (side + 1) * chans]

    def store(number, turn):
        return [
            pltpu.make_async_copy(
                stage.at[turn, side],
                out_ref.at[
                    pl.ds(number * ISTEP, ISTEP), pl.ds(pl.multiple_of(meta_ref[side] * chans, chans), chans)
                ],
                out_sems.at[turn, side],
            )
            for side in range(sides)
        ]

    steps = chans // ISTEP

    @pl.loop(0, steps)
    def _(number):
        turn = lax.rem(number, 2)

        @pl.when(number >= 2)
        def _():
            for copy in store(number - 2, turn):
                copy.wait()

        for side in range(sides):
            for q in range(ISTEP):
                rows = total[side, pl.ds(number * ISTEP + q, bins, stride=pitch), :]
                stage[turn, side, q] = rows.T.astype(jnp.bfloat16)
        for copy in store(number, turn):
            copy.start()

    for number in (steps - 2, steps - 1):
        for copy in store(number, number % 2):
            copy.wait()


def cross_step(lhs, prior, parts, blocks):
    bins, chans, depth = lhs.shape
    sides = len(parts)
    meta = jnp.stack([slot for _, _, slot in parts] + [jnp.asarray(pick) for _, pick, _ in parts]).astype(jnp.int32)
    operands = [meta, lhs] + [value for values, _, _ in parts for value in values]
    aliases = {}
    if prior is not None:
        aliases = {len(operands): 0}
        operands.append(prior)
    return pl.pallas_call(
        functools.partial(cross_kernel, tuple(len(values) for values, _, _ in parts), prior is not None),
        in_specs=[pl.BlockSpec(memory_space=pltpu.SMEM), pl.BlockSpec(memory_space=pltpu.VMEM)]
        + [pl.BlockSpec(memory_space=pl.ANY)] * (len(operands) - 2),
        out_specs=pl.BlockSpec(memory_space=pl.ANY),
        scratch_shapes=[
            pltpu.VMEM((sides, bins, depth // 2, chans), jnp.bfloat16),
            pltpu.VMEM((sides, bins * (chans + SPARE), chans), jnp.float32),
            pltpu.VMEM((2, sides, ISTEP, chans, bins), jnp.bfloat16),
            pltpu.SemaphoreType.DMA((sides, bins // FSTEP)),
            pltpu.SemaphoreType.DMA((2, sides)),
        ],
        out_shape=jax.ShapeDtypeStruct((chans, 2 * chans * blocks, bins), jnp.bfloat16),
        input_output_aliases=aliases,
        compiler_params=pltpu.CompilerParams(vmem_limit_bytes=32 * 2**20),
        cost_estimate=pl.CostEstimate(
            flops=2 * sides * bins * depth * chans * chans,
            bytes_accessed=10 * 2**20 * sides,
            transcendentals=0,
        ),
        name="cross",
    )(*operands)


def joined(keep, other):
    return jnp.transpose(jnp.concatenate([keep, other], axis=0), (1, 0, 2))


def on_line(strain, offsets, bins):
    chans = strain.shape[0]
    share = bins.shape[0] // 2
    keep_a, keep_b, send_a, send_b = own_spectra(
        strain, offsets, jnp.roll(bins, -share * lax.axis_index("band"))
    )
    other_a = lax.ppermute(send_a, "band", [(0, 1), (1, 0)])
    other_b = lax.ppermute(send_b, "band", [(0, 1), (1, 0)])
    a, b = joined(keep_a, other_a), joined(keep_b, other_b)
    me = lax.axis_index("chan")
    z, x = me // 2, me % 2
    middle = (z == 1) | (z == 2)

    def along(value, pairs):
        return lax.ppermute(value, "chan", [(2 * p + s, 2 * q + s) for p, q in pairs for s in range(2)])

    def swap(value):
        return along(value, [(0, 1), (1, 0), (2, 3), (3, 2)])

    def outward(value):
        return along(value, [(1, 0), (2, 3)])

    def inner(value):
        return along(value, [(1, 2), (2, 1)])

    def across(value, rows=range(4)):
        return lax.ppermute(value, "chan", [(2 * a + s, 2 * a + 1 - s) for a in rows for s in range(2)])

    ends, inside = (0, 3), (1, 2)

    def tie(*values):
        return lax.optimization_barrier(values)

    def choose(values):
        return jnp.where(z == 0, values[0], jnp.where(z == 1, values[1], jnp.where(z == 2, values[2], values[3])))

    near, mid, far = choose([1, 0, 3, 2]), choose([2, 2, 1, 1]), choose([3, 3, 0, 0])

    def slot(row, column, half):
        return 2 * (2 * row + column) + half

    def cross(prior, *parts):
        return cross_step(lhs, prior, parts, 8)

    def one(value, *place):
        return (value,), 0, slot(*place)

    def either(at_end, at_middle, *place):
        return (at_end, at_middle), middle, slot(*place)

    def mixed(at_end, at_middle, end_place, middle_place):
        return (at_end, at_middle), middle, jnp.where(middle, slot(*middle_place), slot(*end_place))

    near_a, in1_a, side_a = swap(a), inner(a), across(a)
    near_b, side_b = swap(b), across(b)
    lhs = turn_own(a, b)
    out = cross(None, one(a, z, x, 0), one(b, z, x, 1))
    near_a, in1_a, side_a, b, out = tie(near_a, in1_a, side_a, b, out)

    out2_a, near_xa, in1_b = outward(in1_a), across(near_a), inner(b)
    out = cross(out, one(side_a, z, 1 - x, 0), one(near_a, near, x, 0))
    near_a, near_b, side_a, side_b, in1_b, out = tie(near_a, near_b, side_a, side_b, in1_b, out)

    out2_b, in2_a, in2_b = outward(in1_b), inner(near_a), inner(near_b)
    out = cross(out, one(side_b, z, 1 - x, 1), one(near_b, near, x, 1))
    out2_a, out = tie(out2_a, out)

    mid_xa_e = across(out2_a, ends)
    near_xa, in2_a, side_a, out = tie(near_xa, in2_a, side_a, out)
    out3_a, mid_xa_m = outward(in2_a), inner(side_a)
    out = cross(out, either(out2_a, in1_a, mid, x, 0), one(near_xa, near, 1 - x, 0))
    out2_b, in2_b, in2_a, out = tie(out2_b, in2_b, in2_a, out)

    mid_xb_e = across(out2_b, ends)
    mid_xa_e, in2_b, in2_a, out = tie(mid_xa_e, in2_b, in2_a, out)
    out3_b, far_xa_m = outward(in2_b), across(in2_a, inside)
    out = cross(out, either(out2_b, in1_b, mid, x, 1), mixed(mid_xa_e, in2_a, (mid, 1 - x, 0), (far, x, 0)))
    out3_a, mid_xa_m, side_b, out = tie(out3_a, mid_xa_m, side_b, out)

    far_xa_e, mid_xb_m = across(out3_a, ends), inner(side_b)
    mid_xb_e, far_xa_m, side_b, in2_b, out = tie(mid_xb_e, far_xa_m, side_b, in2_b, out)
    near_xb, far_xb_m = swap(side_b), across(in2_b, inside)
    out = cross(
        out,
        mixed(out3_a, mid_xa_m, (far, x, 0), (mid, 1 - x, 0)),
        mixed(mid_xb_e, in2_b, (mid, 1 - x, 1), (far, x, 1)),
    )
    out3_b, out = tie(out3_b, out)

    far_xb_e = across(out3_b, ends)
    far_xa_e, mid_xb_m, out = tie(far_xa_e, mid_xb_m, out)
    out = cross(
        out,
        mixed(out3_b, mid_xb_m, (far, x, 1), (mid, 1 - x, 1)),
        either(far_xa_e, far_xa_m, far, 1 - x, 0),
    )
    near_xb, out = tie(near_xb, out)
    out = cross(out, one(near_xb, near, 1 - x, 1))
    far_xb_e, far_xb_m, out = tie(far_xb_e, far_xb_m, out)
    out = cross(out, either(far_xb_e, far_xb_m, far, 1 - x, 1))
    return out.reshape(chans, 8 * chans, 2, share)


def on_device(strain, offsets, bins):
    if strain.shape[0] == 128 and lax.axis_size("chan") == 8 and bins.shape[0] // lax.axis_size("band") == 128:
        return on_line(strain, offsets, bins)
    return on_any(strain, offsets, bins)


def solution(mesh):
    placed = (P(("seg", "chan"), "band", None), P(("seg", "band"), None), P())
    return jax.shard_map(
        on_device,
        mesh=mesh,
        in_specs=placed,
        out_specs=P(("seg", "chan"), None, None, "band"),
        check_vma=False,
    )
```

```python
import functools
import math

import jax
import jax.numpy as jnp
from jax import lax
from jax.experimental import pallas as pl
from jax.experimental.pallas import tpu as pltpu
from jax.sharding import PartitionSpec as P

WIN_LEN = 1000
GROUP = 128
REACH = 64


def normalize(strain):
    samples = strain.shape[2]
    padded = jnp.pad(jnp.abs(strain), ((0, 0), (0, 0), (REACH, REACH)))
    total, reach = padded, 1
    while reach < 2 * REACH:
        total = total[:, :, : total.shape[2] - reach] + total[:, :, reach:]
        reach *= 2
    running = total[:, :, :samples] + padded[:, :, 2 * REACH :]
    pos = jnp.arange(samples)
    counts = jnp.minimum(pos + REACH, samples - 1) - jnp.maximum(pos - REACH, 0) + 1
    return strain / (running / counts.astype(strain.dtype) + 1e-06)


def cut_windows(normed, offsets):

    def one_file(rows, starts):
        return jax.vmap(lambda start_pos: lax.dynamic_slice_in_dim(rows, start_pos, WIN_LEN, 1))(
            starts
        )

    pieces = jax.vmap(one_file, in_axes=(1, 0))(normed, offsets)
    sample_pos = jnp.arange(WIN_LEN, dtype=jnp.float32)
    hann_taper = 0.5 - 0.5 * jnp.cos(2.0 * math.pi * (sample_pos + 0.5) / WIN_LEN)
    return (jnp.transpose(pieces, (2, 0, 1, 3)) * hann_taper).astype(jnp.bfloat16)


def make_table(bins):
    sample_idx = jnp.arange(WIN_LEN, dtype=jnp.int32)
    phase_idx = sample_idx[:, None] * bins[None, :] % WIN_LEN
    angles = phase_idx.astype(jnp.float32) * (2.0 * math.pi / WIN_LEN)
    return jnp.concatenate([jnp.cos(angles), -jnp.sin(angles)], axis=1).astype(jnp.bfloat16)


def spectra(windows, table):
    flat_rows = windows.reshape(-1, WIN_LEN)
    result = jnp.dot(flat_rows, table, preferred_element_type=jnp.float32)
    return result.reshape(
        windows.shape[0], windows.shape[1] * windows.shape[2], 2, table.shape[1] // 2
    )


def whiten(spec):
    chan_rows, win_count, _, bin_count = spec.shape
    grouped = spec.reshape(chan_rows, win_count, 2, bin_count // GROUP, GROUP)
    power_mean = jnp.mean(jnp.sum(grouped * grouped, axis=2), axis=-1, keepdims=True)
    gain_inv = lax.rsqrt(power_mean + 1e-06)[:, :, None]
    return (grouped * gain_inv).reshape(spec.shape).astype(jnp.bfloat16)


def cross_block(lhs_rows, other, win_count):
    products = jnp.einsum("iwcf,jwcf->ijf", lhs_rows, other, preferred_element_type=jnp.float32)
    chan_rows = lhs_rows.shape[0] // 2
    split_parts = products.reshape(2, chan_rows, other.shape[0], products.shape[2])
    return (jnp.transpose(split_parts, (1, 2, 0, 3)) / win_count).astype(jnp.bfloat16)


def on_any(strain, offsets, bins):
    normed = normalize(strain)
    windows = cut_windows(normed, offsets)
    band_count = lax.axis_size("band")
    bin_share = bins.shape[0] // band_count
    all_windows = lax.all_gather(windows, "band", axis=1, tiled=True)
    my_bins = lax.dynamic_slice_in_dim(bins, lax.axis_index("band") * bin_share, bin_share)
    whitened = whiten(spectra(all_windows, make_table(my_bins)))
    chan_rows = whitened.shape[0]
    win_count = whitened.shape[1]
    rotated = jnp.stack([whitened[:, :, 1], -whitened[:, :, 0]], axis=2)
    lhs_rows = jnp.concatenate([whitened, rotated], axis=0)
    chan_count = lax.axis_size("chan")
    col_count = chan_rows * chan_count
    blank_out = jnp.zeros((chan_rows, col_count, 2, bin_share), jnp.bfloat16)
    return lax.dynamic_update_slice_in_dim(
        blank_out,
        cross_block(lhs_rows, lax.all_gather(whitened, "chan", axis=0, tiled=True), win_count),
        jnp.int32(0),
        1,
    )


def round_up(size, step):
    return -(-size // step) * step


BLOCK = 120


def fill_table(bins_ref, table):
    step = 8
    sample = lax.broadcasted_iota(jnp.int32, (step, table.shape[1]), 1)
    inside = sample < WIN_LEN
    sample = sample.astype(jnp.float32)
    per = GROUP // (2 * step)

    @pl.loop(0, bins_ref.shape[0] // (2 * step), unroll=4)
    def _(block):
        cos_rows, sin_rows = [], []
        for q in range(2):
            at = pl.multiple_of((2 * block + q) * step, step)
            product = bins_ref[pl.ds(at, step), :][:, :1] * sample
            quarter = jnp.floor(product * (4.0 / WIN_LEN) + 0.5)
            angle = (product - quarter * (WIN_LEN // 4)) * (2.0 * math.pi / WIN_LEN)
            square = angle * angle
            sin = angle * (1.0 + square * (-1 / 6 + square * (1 / 120 + square * (-1 / 5040 + square * (1 / 362880)))))
            cos = 1.0 + square * (-1 / 2 + square * (1 / 24 + square * (-1 / 720 + square * (1 / 40320))))
            quarter = quarter - 4.0 * jnp.floor(quarter * 0.25)
            odd = (quarter == 1.0) | (quarter == 3.0)
            real = jnp.where(odd, sin, cos)
            imag = jnp.where(odd, cos, sin)
            real = jnp.where((quarter == 1.0) | (quarter == 2.0), -real, real)
            imag = jnp.where(quarter >= 2.0, imag, -imag)
            cos_rows.append(jnp.where(inside, real, 0.0).astype(jnp.bfloat16))
            sin_rows.append(jnp.where(inside, imag, 0.0).astype(jnp.bfloat16))
        first = pl.multiple_of((block // per) * 2 * GROUP + lax.rem(block, per) * 2 * step, 2 * step)
        table[pl.ds(first, 2 * step), :] = jnp.concatenate(cos_rows, axis=0)
        table[pl.ds(first + GROUP, 2 * step), :] = jnp.concatenate(sin_rows, axis=0)


def sum_eight(low, rows, mags, eights):
    total, reach = mags[pl.ds(low, rows + 8), :], 1
    while reach < 8:
        total = total + pltpu.roll(total, rows + 8 - reach, 0)
        reach *= 2
    eights[pl.ds(low, rows), :] = total[:rows]


def sum_four(low, rows, step, source):
    return (source[pl.ds(low, rows), :] + source[pl.ds(low + step, rows), :]) + (
        source[pl.ds(low + 2 * step, rows), :] + source[pl.ds(low + 3 * step, rows), :]
    )


def normalize_block(low, rows, source, mags, wides, normed):
    samples, chans = source.shape
    total = sum_four(low, rows, 32, wides) + mags[pl.ds(low + 2 * REACH, rows), :]
    if low >= REACH and low + rows + REACH <= samples:
        mean = total * (1.0 / (2 * REACH + 1))
    else:
        pos = lax.broadcasted_iota(jnp.int32, (rows, chans), 0) + low
        counts = jnp.minimum(pos + REACH, samples - 1) - jnp.maximum(pos - REACH, 0) + 1
        mean = total / counts.astype(jnp.float32)
    normed[pl.ds(low, rows), :] = source[pl.ds(low, rows), :] / (mean + 1e-06)


def spectra_kernel(offs_ref, strain_ref, hann_ref, bins_ref, keep_a, keep_b, send_a, send_b, strain, mags, eights, wides, normed, table, sems):
    files, samples, chans = strain.shape
    win_file = offs_ref.shape[1]
    depth = table.shape[1]
    half = chans // 2
    copies = [pltpu.make_async_copy(strain_ref.at[m], strain.at[m], sems.at[m]) for m in range(files)]
    for copy in copies:
        copy.start()
    for m in range(2):
        tail = mags.shape[1] - REACH - samples
        mags[m, pl.ds(0, REACH), :] = jnp.zeros((REACH, chans), jnp.float32)
        mags[m, pl.ds(REACH + samples, tail), :] = jnp.zeros((tail, chans), jnp.float32)
    for m in range(files):
        spare = normed.shape[1] - samples
        normed[m, pl.ds(samples, spare), :] = jnp.zeros((spare, chans), jnp.float32)
    fill_table(bins_ref, table)

    def blocks(rows):
        return [(low, min(BLOCK, rows - low)) for low in range(0, rows, BLOCK)]

    def prepare(m):
        own, source = mags.at[m % 2], strain.at[m]

        def load():
            copies[m].wait()
            own[pl.ds(REACH, samples), :] = jnp.abs(source[...])

        def wide(low, rows):
            wides[pl.ds(low, rows), :] = sum_four(low, rows, 8, eights)

        return (
            [load]
            + [functools.partial(sum_eight, low, rows, own, eights) for low, rows in blocks(samples + 120)]
            + [functools.partial(wide, low, rows) for low, rows in blocks(samples + 96)]
            + [
                functools.partial(normalize_block, low, rows, source, own, wides, normed.at[m])
                for low, rows in blocks(samples)
            ]
        )

    for piece in prepare(0):
        piece()
    pairs = win_file // 2
    left = lax.broadcasted_iota(jnp.int32, (GROUP, chans), 1) < half
    for m in range(files):
        for pair in range(pairs):
            pieces = prepare(m + 1) if m + 1 < files else []
            for piece in pieces[len(pieces) * pair // pairs : len(pieces) * (pair + 1) // pairs]:
                piece()
            wins = [
                (normed[m, pl.ds(offs_ref[m, 2 * pair + e], depth), :] * hann_ref[...]).astype(jnp.bfloat16)
                for e in range(2)
            ]
            spec = jnp.dot(table[...], jnp.concatenate(wins, axis=1), preferred_element_type=jnp.float32)
            for g, (out_a, out_b) in enumerate(((keep_a, keep_b), (send_a, send_b))):
                part = spec[g * 2 * GROUP : (g + 1) * 2 * GROUP]
                power = jnp.sum(part * part, axis=0, keepdims=True) / GROUP
                part = part * lax.rsqrt(power + 1e-06)
                for e in range(2):
                    real = part[:GROUP, e * chans : (e + 1) * chans]
                    imag = part[GROUP:, e * chans : (e + 1) * chans]
                    at = m * win_file + 2 * pair + e
                    out_a[at] = jnp.where(left, real, pltpu.roll(imag, half, 1)).astype(jnp.bfloat16)
                    out_b[at] = jnp.where(left, pltpu.roll(real, half, 1), imag).astype(jnp.bfloat16)


def own_spectra(strain, offsets, bins):
    chans, files, samples = strain.shape
    wins = files * offsets.shape[1]
    depth = round_up(WIN_LEN, 128)
    sample_pos = jnp.arange(WIN_LEN, dtype=jnp.float32)
    taper = 0.5 - 0.5 * jnp.cos(2.0 * math.pi * (sample_pos + 0.5) / WIN_LEN)
    taper = jnp.broadcast_to(jnp.pad(taper, (0, depth - WIN_LEN))[:, None], (depth, chans))
    rows = jnp.broadcast_to(bins.astype(jnp.float32)[:, None], (bins.shape[0], 128))
    whole = pl.BlockSpec(memory_space=pltpu.VMEM)
    shape = jax.ShapeDtypeStruct((wins, GROUP, chans), jnp.bfloat16)
    return pl.pallas_call(
        spectra_kernel,
        in_specs=[pl.BlockSpec(memory_space=pltpu.SMEM), pl.BlockSpec(memory_space=pl.ANY), whole, whole],
        out_specs=[whole] * 4,
        scratch_shapes=[
            pltpu.VMEM((files, samples, chans), jnp.float32),
            pltpu.VMEM((2, round_up(samples + 2 * REACH, 8), chans), jnp.float32),
            pltpu.VMEM((samples + 120, chans), jnp.float32),
            pltpu.VMEM((samples + 96, chans), jnp.float32),
            pltpu.VMEM((files, round_up(samples - WIN_LEN + depth, 8), chans), jnp.float32),
            pltpu.VMEM((2 * bins.shape[0], depth), jnp.bfloat16),
            pltpu.SemaphoreType.DMA((files,)),
        ],
        out_shape=[shape] * 4,
        compiler_params=pltpu.CompilerParams(vmem_limit_bytes=48 * 2**20),
        name="spectra",
    )(offsets, jnp.transpose(strain, (1, 2, 0)), taper, rows)


FSTEP = 16
ISTEP = 32
SPARE = 8


def turn_kernel(first_ref, second_ref, out_ref):
    bins, wins, chans = first_ref.shape
    half = chans // 2
    left = lax.broadcasted_iota(jnp.int32, (wins, chans), 1) < half
    for q in range(bins):
        first = first_ref[q].astype(jnp.float32)
        second = second_ref[q].astype(jnp.float32)
        real = jnp.where(left, first, pltpu.roll(second, half, 1))
        imag = jnp.where(left, pltpu.roll(first, half, 1), second)
        out_ref[q] = jnp.concatenate([real, imag], axis=0).T.astype(jnp.bfloat16)


def turn_own(first, second):
    bins, wins, chans = first.shape
    spec = pl.BlockSpec((FSTEP, wins, chans), lambda i: (i, 0, 0))
    return pl.pallas_call(
        turn_kernel,
        grid=(bins // FSTEP,),
        in_specs=[spec, spec],
        out_specs=pl.BlockSpec((FSTEP, chans, 2 * wins), lambda i: (i, 0, 0)),
        out_shape=jax.ShapeDtypeStruct((bins, chans, 2 * wins), jnp.bfloat16),
        cost_estimate=pl.CostEstimate(flops=10**6, bytes_accessed=8 * 2**20, transcendentals=0),
        name="turn",
    )(first, second)


def cross_kernel(counts, has_prior, meta_ref, lhs_ref, *rest):
    sides = len(counts)
    groups = []
    for count in counts:
        groups.append(rest[:count])
        rest = rest[count:]
    if has_prior:
        rest = rest[1:]
    out_ref, held, total, stage, in_sems, out_sems = rest
    bins, chans, depth = lhs_ref.shape
    wins = depth // 2
    pitch = chans + SPARE
    parts = bins // FSTEP

    def rows_of(part):
        return pl.ds(part * FSTEP, FSTEP)

    def held_copy(side, ref, part):
        return pltpu.make_async_copy(ref.at[rows_of(part)], held.at[side, rows_of(part)], in_sems.at[side, part])

    for part in range(parts):
        for side, refs in enumerate(groups):
            if len(refs) == 1:
                held_copy(side, refs[0], part).start()
            for n, ref in enumerate(refs if len(refs) > 1 else ()):

                @pl.when(meta_ref[sides + side] == n)
                def _():
                    held_copy(side, ref, part).start()

    lane = lax.broadcasted_iota(jnp.int32, (FSTEP * wins, chans), 1)
    odd = lane % 2
    straight = lane // 2 + odd * (chans // 2)
    crossed = lane // 2 + (1 - odd) * (chans // 2)
    sign = (1 - 2 * odd).astype(jnp.float32)

    @pl.loop(0, parts)
    def _(part):
        base = part * FSTEP
        mixed = []
        for side in range(sides):
            held_copy(side, groups[side][0], part).wait()
            rows = held[side, pl.ds(base, FSTEP)].reshape(FSTEP * wins, chans).astype(jnp.float32)
            upper = jnp.take_along_axis(rows, straight, axis=1) * sign
            lower = jnp.take_along_axis(rows, crossed, axis=1)
            mixed.append(
                jnp.concatenate(
                    [piece.astype(jnp.bfloat16).reshape(FSTEP, wins, chans) for piece in (upper, lower)], axis=1
                )
            )
        for q in range(FSTEP):
            rhs = jnp.concatenate([piece[q] for piece in mixed], axis=1)
            prod = jnp.dot(lhs_ref[base + q], rhs, preferred_element_type=jnp.float32) * (1.0 / wins)
            at = pl.ds(pl.multiple_of((base + q) * pitch, 8), chans)
            for side in range(sides):
                total[side, at, :] = prod[:, side * chans : (side + 1) * chans]

    def store(number, turn):
        return [
            pltpu.make_async_copy(
                stage.at[turn, side],
                out_ref.at[
                    pl.ds(number * ISTEP, ISTEP), pl.ds(pl.multiple_of(meta_ref[side] * chans, chans), chans)
                ],
                out_sems.at[turn, side],
            )
            for side in range(sides)
        ]

    steps = chans // ISTEP

    @pl.loop(0, steps)
    def _(number):
        turn = lax.rem(number, 2)

        @pl.when(number >= 2)
        def _():
            for copy in store(number - 2, turn):
                copy.wait()

        for side in range(sides):
            for q in range(ISTEP):
                rows = total[side, pl.ds(number * ISTEP + q, bins, stride=pitch), :]
                stage[turn, side, q] = rows.T.astype(jnp.bfloat16)
        for copy in store(number, turn):
            copy.start()

    for number in (steps - 2, steps - 1):
        for copy in store(number, number % 2):
            copy.wait()


def cross_step(lhs, prior, parts, blocks):
    bins, chans, depth = lhs.shape
    sides = len(parts)
    meta = jnp.stack([slot for _, _, slot in parts] + [jnp.asarray(pick) for _, pick, _ in parts]).astype(jnp.int32)
    operands = [meta, lhs] + [value for values, _, _ in parts for value in values]
    aliases = {}
    if prior is not None:
        aliases = {len(operands): 0}
        operands.append(prior)
    return pl.pallas_call(
        functools.partial(cross_kernel, tuple(len(values) for values, _, _ in parts), prior is not None),
        in_specs=[pl.BlockSpec(memory_space=pltpu.SMEM), pl.BlockSpec(memory_space=pltpu.VMEM)]
        + [pl.BlockSpec(memory_space=pl.ANY)] * (len(operands) - 2),
        out_specs=pl.BlockSpec(memory_space=pl.ANY),
        scratch_shapes=[
            pltpu.VMEM((sides, bins, depth // 2, chans), jnp.bfloat16),
            pltpu.VMEM((sides, bins * (chans + SPARE), chans), jnp.float32),
            pltpu.VMEM((2, sides, ISTEP, chans, bins), jnp.bfloat16),
            pltpu.SemaphoreType.DMA((sides, bins // FSTEP)),
            pltpu.SemaphoreType.DMA((2, sides)),
        ],
        out_shape=jax.ShapeDtypeStruct((chans, 2 * chans * blocks, bins), jnp.bfloat16),
        input_output_aliases=aliases,
        compiler_params=pltpu.CompilerParams(vmem_limit_bytes=32 * 2**20),
        cost_estimate=pl.CostEstimate(
            flops=2 * sides * bins * depth * chans * chans,
            bytes_accessed=10 * 2**20 * sides,
            transcendentals=0,
        ),
        name="cross",
    )(*operands)


def joined(keep, other):
    return jnp.transpose(jnp.concatenate([keep, other], axis=0), (1, 0, 2))


def on_line(strain, offsets, bins):
    chans = strain.shape[0]
    share = bins.shape[0] // 2
    keep_a, keep_b, send_a, send_b = own_spectra(
        strain, offsets, jnp.roll(bins, -share * lax.axis_index("band"))
    )
    other_a = lax.ppermute(send_a, "band", [(0, 1), (1, 0)])
    other_b = lax.ppermute(send_b, "band", [(0, 1), (1, 0)])
    a, b = joined(keep_a, other_a), joined(keep_b, other_b)
    me = lax.axis_index("chan")
    z, x = me // 2, me % 2
    middle = (z == 1) | (z == 2)

    def along(value, pairs):
        return lax.ppermute(value, "chan", [(2 * p + s, 2 * q + s) for p, q in pairs for s in range(2)])

    def swap(value):
        return along(value, [(0, 1), (1, 0), (2, 3), (3, 2)])

    def outward(value):
        return along(value, [(1, 0), (2, 3)])

    def inner(value):
        return along(value, [(1, 2), (2, 1)])

    def across(value, rows=range(4)):
        return lax.ppermute(value, "chan", [(2 * a + s, 2 * a + 1 - s) for a in rows for s in range(2)])

    ends, inside = (0, 3), (1, 2)

    def tie(*values):
        return lax.optimization_barrier(values)

    def choose(values):
        return jnp.where(z == 0, values[0], jnp.where(z == 1, values[1], jnp.where(z == 2, values[2], values[3])))

    near, mid, far = choose([1, 0, 3, 2]), choose([2, 2, 1, 1]), choose([3, 3, 0, 0])

    def slot(row, column, half):
        return 2 * (2 * row + column) + half

    def cross(prior, *parts):
        return cross_step(lhs, prior, parts, 8)

    def one(value, *place):
        return (value,), 0, slot(*place)

    def either(at_end, at_middle, *place):
        return (at_end, at_middle), middle, slot(*place)

    def mixed(at_end, at_middle, end_place, middle_place):
        return (at_end, at_middle), middle, jnp.where(middle, slot(*middle_place), slot(*end_place))

    near_a, in1_a, side_a = swap(a), inner(a), across(a)
    near_b, side_b = swap(b), across(b)
    lhs = turn_own(a, b)
    out = cross(None, one(a, z, x, 0), one(b, z, x, 1))
    near_a, in1_a, side_a, b, out = tie(near_a, in1_a, side_a, b, out)

    out2_a, near_xa, in1_b = outward(in1_a), across(near_a), inner(b)
    out = cross(out, one(side_a, z, 1 - x, 0), one(near_a, near, x, 0))
    near_a, near_b, side_a, side_b, in1_b, out = tie(near_a, near_b, side_a, side_b, in1_b, out)

    out2_b, in2_a, in2_b = outward(in1_b), inner(near_a), inner(near_b)
    out = cross(out, one(side_b, z, 1 - x, 1), one(near_b, near, x, 1))
    out2_a, out = tie(out2_a, out)

    mid_xa_e = across(out2_a, ends)
    near_xa, in2_a, side_a, out = tie(near_xa, in2_a, side_a, out)
    out3_a, mid_xa_m = outward(in2_a), inner(side_a)
    out = cross(out, either(out2_a, in1_a, mid, x, 0), one(near_xa, near, 1 - x, 0))
    out2_b, in2_b, in2_a, out = tie(out2_b, in2_b, in2_a, out)

    mid_b = jnp.where(middle, in1_b, out2_b)
    mid_xb = across(mid_b)
    mid_xa_e, mid_b, in2_b, in2_a, out = tie(mid_xa_e, mid_b, in2_b, in2_a, out)
    out3_b, far_xa_m = outward(in2_b), across(in2_a, inside)
    out = cross(out, one(mid_b, mid, x, 1), mixed(mid_xa_e, in2_a, (mid, 1 - x, 0), (far, x, 0)))
    out3_a, mid_xa_m, side_b, out = tie(out3_a, mid_xa_m, side_b, out)

    far_xa_e = across(out3_a, ends)
    mid_xb, side_b, in2_b, out = tie(mid_xb, side_b, in2_b, out)
    near_xb, far_xb_m = swap(side_b), across(in2_b, inside)
    out = cross(out, mixed(out3_a, mid_xa_m, (far, x, 0), (mid, 1 - x, 0)), one(mid_xb, mid, 1 - x, 1))
    out3_b, out = tie(out3_b, out)

    far_xb_e = across(out3_b, ends)
    far_xa_e, far_xa_m, out = tie(far_xa_e, far_xa_m, out)
    out = cross(out, either(out3_b, in2_b, far, x, 1), either(far_xa_e, far_xa_m, far, 1 - x, 0))
    near_xb, out = tie(near_xb, out)
    out = cross(out, one(near_xb, near, 1 - x, 1))
    far_xb_e, far_xb_m, out = tie(far_xb_e, far_xb_m, out)
    out = cross(out, either(far_xb_e, far_xb_m, far, 1 - x, 1))
    return out.reshape(chans, 8 * chans, 2, share)


def on_device(strain, offsets, bins):
    if strain.shape[0] == 128 and lax.axis_size("chan") == 8 and bins.shape[0] // lax.axis_size("band") == 128:
        return on_line(strain, offsets, bins)
    return on_any(strain, offsets, bins)


def solution(mesh):
    placed = (P(("seg", "chan"), "band", None), P(("seg", "band"), None), P())
    return jax.shard_map(
        on_device,
        mesh=mesh,
        in_specs=placed,
        out_specs=P(("seg", "chan"), None, None, "band"),
        check_vma=False,
    )
```
